32 devices in a mesh: view: 8 (over z, x), img: 4 (over y, core).
Axes of the slice: x: 2, y: 2, z: 4, core: 2. Of those that a mesh axis runs over, the one named last changes fastest.
Arguments:
- volume: bfloat16 [128, 128, 2048], P('view', 'img'), may hold values from -6 to 6
- occupied: int32 [8, 4, 16], P('view', 'img'), may hold values from -1 to 15, as said below
- sample_counts: int32 [8, 4, 16], P('view', 'img'), may hold values from 6 to 24, as said below
- depth_order: int32 [8], replicated, may hold values from 0 to 7, each once
- colors: bfloat16 [3, 128], replicated, may hold values from 0.049804688 to 1
- density: bfloat16 [128], replicated, may hold values from 0.0019989014 to 0.039794922
Outputs:
- frame: float32 [4, 128, 2048], P(None, 'img', 'view')
The draws below stay inside these ranges and needn't reach their ends.
Inputs may be any that keep to these rules, and one draw needn't show every extreme that they name: `occupied`: each brick's list names distinct tiles of 0..15 first and then holds -1; a brick lists 16, half, a quarter or an eighth of its tiles (at least 2), and some brick lists all of them. `sample_counts`: every brick has a tile with 24 samples. `depth_order`: A permutation of the bricks along view.
All inputs are finite; a program needn't handle non-finite values.
Results may differ from the reference program's by a relative error of at most 0.0003.
Values may be sent and summed in bfloat16 or wider, within the bound.
A program may use at most 64 MiB of HBM per device.

```python
import math
import jax
import jax.numpy as jnp
from jax import lax

SLICES = 16
ROWS = 32
COLS = 2048
TILE_COLS = 128
SAMPLE_MAX = 24
BINS = 128
SAMPLE_MIN = 6
TILES_DEV = 16
DEPTH = 128
FRAME_ROWS = 128
N_VIEW = 8
N_IMG = 4


def draw_occupied(key, part):
    bricks = N_VIEW * N_IMG
    key_drop, key_full, key_order = jax.random.split(jax.random.fold_in(key, 101), 3)
    halvings = jax.random.randint(key_drop, (bricks,), 0, 4)
    fullest = jax.random.randint(key_full, (), 0, bricks)
    halvings = jnp.where(jnp.arange(bricks) == fullest, 0, halvings)
    listed_count = jnp.maximum(jnp.right_shift(jnp.int32(TILES_DEV), halvings), 2)
    shuffled = jax.vmap(lambda inner: jax.random.permutation(inner, TILES_DEV))(jax.random.split(key_order, bricks))
    chosen = jnp.where(jnp.arange(TILES_DEV)[None, :] < listed_count[:, None], shuffled, -1)
    return chosen.reshape(N_VIEW, N_IMG, TILES_DEV).astype(jnp.int32)


def draw_sample_counts(key, part):
    bricks = N_VIEW * N_IMG
    key_count, key_top = jax.random.split(jax.random.fold_in(key, 202))
    drawn = jax.random.randint(key_count, (bricks, TILES_DEV), SAMPLE_MIN, SAMPLE_MAX + 1)
    topmost = jax.random.randint(key_top, (bricks, 1), 0, TILES_DEV)
    drawn = jnp.where(jnp.arange(TILES_DEV)[None, :] == topmost, SAMPLE_MAX, drawn)
    return drawn.reshape(N_VIEW, N_IMG, TILES_DEV).astype(jnp.int32)


def level_of(stream_key, extent, cuts, low, largest):
    factor_of, own = 1.0, jax.random.fold_in(stream_key, 6)
    for dim, shards_of in cuts:
        steps = jnp.exp(jax.random.uniform(jax.random.fold_in(own, dim), (shards_of,), jnp.float32, low / len(cuts), largest / len(cuts)))
        factor_of = factor_of * jnp.repeat(steps, extent[dim] // shards_of).reshape([-1 if axis == dim else 1 for axis in range(len(extent))])
    return factor_of


def normal_values(own_key, extent, spread, reach, shards=(), held_as=jnp.bfloat16):
    values = jax.random.normal(own_key, extent, jnp.float32) * spread
    if len(shards) > 0:
        values = level_of(own_key, extent, shards, -0.22, 0.18) * values
    return jnp.clip(values, min=-reach, max=reach).astype(held_as)


def setup_inputs(seed: int = 0) -> dict:
    key_list = jax.random.split(jax.random.key(seed), 7)
    volume = normal_values(key_list[0], (DEPTH, FRAME_ROWS, COLS), 1.0, 6.0, ((0, 8), (1, 4)))
    occupied = draw_occupied(jax.random.fold_in(key_list[6], 71), 0)
    sample_counts = draw_sample_counts(jax.random.fold_in(key_list[6], 71), 0)
    depth_order = jax.random.permutation(key_list[3], N_VIEW).astype(jnp.int32)
    colors = jnp.clip(jax.random.uniform(key_list[4], (3, BINS), jnp.float32, 0.049804688, 1.0), 0.049804688, 1.0).astype(jnp.bfloat16)
    density = jnp.clip(jnp.exp(jax.random.uniform(key_list[5], (BINS,), jnp.float32, math.log(0.0019989014), math.log(0.039794922))), 0.0019989014, 0.039794922).astype(jnp.bfloat16)
    return dict(volume=volume, occupied=occupied, sample_counts=sample_counts, depth_order=depth_order, colors=colors, density=density)


def tent(offset):
    return jnp.maximum(0.0, 1.0 - jnp.abs(offset))


def reference(volume, occupied, sample_counts, depth_order, colors, density):
    table = jnp.concatenate([colors, density[None, :]], axis=0)
    zero_slice = jnp.zeros((1, FRAME_ROWS, COLS), volume.dtype)
    padded = jnp.pad(jnp.concatenate([volume, zero_slice], axis=0), ((0, 0), (1, 1), (1, 1)))
    tile_of_column = jnp.arange(COLS, dtype=jnp.int32) // TILE_COLS
    slice_index = jnp.arange(SLICES + 1, dtype=jnp.float32)
    bin_index = jnp.arange(BINS, dtype=jnp.float32)[:, None]
    tile_index = jnp.arange(TILES_DEV, dtype=jnp.int32)

    def march_brick(brick):
        view_pos = (brick // N_IMG).astype(jnp.int32)
        group_pos = (brick % N_IMG).astype(jnp.int32)
        anchor = jnp.zeros((), jnp.int32)
        cube = lax.dynamic_slice(padded, ((view_pos * SLICES).astype(jnp.int32), (group_pos * ROWS).astype(jnp.int32), anchor), (SLICES + 1, ROWS + 2, COLS + 2)).astype(jnp.float32)
        across = (cube[:, 2:, 1:-1] - cube[:, :-2, 1:-1]) * 0.5
        along = (cube[:, 1:-1, 2:] - cube[:, 1:-1, :-2]) * 0.5
        grads = across * across + along * along
        values = cube[:, 1:-1, 1:-1]
        listed = lax.dynamic_slice(occupied, (view_pos, group_pos, anchor), (1, 1, TILES_DEV))[0, 0]
        counted = lax.dynamic_slice(sample_counts, (view_pos, group_pos, anchor), (1, 1, TILES_DEV))[0, 0]
        present = jnp.any(listed[None, :] == tile_index[:, None], axis=1)
        column_count = counted[tile_of_column]
        column_live = present[tile_of_column]
        count_float = column_count.astype(jnp.float32)

        def sample(carry, number):
            paint, cover, remain = carry
            position = (number.astype(jnp.float32) + 1.0) * SLICES / count_float
            weights_z = tent(position[None, :] - slice_index[:, None])
            sampled = jnp.einsum("jc,jrc->rc", weights_z, values, precision=lax.Precision.HIGHEST)
            sampled_grad = jnp.einsum("jc,jrc->rc", weights_z, grads, precision=lax.Precision.HIGHEST)
            levels = jax.nn.sigmoid(sampled) * (BINS - 1)
            lookup = tent(levels.reshape(1, -1) - bin_index).astype(jnp.bfloat16)
            looked = jnp.dot(table, lookup, preferred_element_type=jnp.float32).reshape(4, ROWS, COLS)
            shading = 0.4 + 0.6 * sampled_grad / (1.0 + sampled_grad)
            opacity = 1.0 - jnp.exp(-(looked[3] * SLICES / count_float))
            live_now = jnp.logical_and(number < column_count, column_live)
            opacity = jnp.where(live_now[None, :], opacity, 0.0)
            weight = remain * opacity
            paint = paint + weight * shading * looked[0:3]
            cover = cover + weight
            remain = remain * (1.0 - opacity)
            return (paint, cover, remain), None

        start = (jnp.zeros((3, ROWS, COLS), jnp.float32), jnp.zeros((ROWS, COLS), jnp.float32), jnp.ones((ROWS, COLS), jnp.float32))
        finished, unused = lax.scan(sample, start, jnp.arange(SAMPLE_MAX, dtype=jnp.int32))
        return jnp.concatenate([finished[0], finished[1][None]], axis=0)

    partials = lax.map(march_brick, jnp.arange(N_VIEW * N_IMG, dtype=jnp.int32))
    layers = partials.reshape(N_VIEW, N_IMG, 4, ROWS, COLS).transpose(0, 2, 1, 3, 4).reshape(N_VIEW, 4, FRAME_ROWS, COLS)

    def blend(position, carry):
        image, remain = carry
        chosen = lax.dynamic_index_in_dim(layers, depth_order[position], 0, keepdims=False)
        return image + remain[None] * chosen, remain * (1.0 - chosen[3])

    image, remain = lax.fori_loop(0, N_VIEW, blend, (jnp.zeros((4, FRAME_ROWS, COLS), jnp.float32), jnp.ones((FRAME_ROWS, COLS), jnp.float32)))
    return image
```

```python
import functools
import math

import jax
import jax.numpy as jnp
from jax import lax
from jax.experimental import pallas as pl
from jax.experimental.pallas import tpu as pltpu
from jax.sharding import PartitionSpec as P

LANES = 128
GROUP = 4
PAD = 8


def gather_lanes(row, index):
    return jnp.take_along_axis(row, index, axis=1, mode="promise_in_bounds")


def rounded(value):
    return value.astype(jnp.bfloat16).astype(jnp.float32)


def prepare_tile(tile, vol, nxt, low, high, vals, grads):
    slices, rows, columns = vol.shape
    start = pl.multiple_of(tile * LANES, LANES)
    before = pl.multiple_of(jnp.maximum(tile - 1, 0) * LANES, LANES)
    after = pl.multiple_of(jnp.minimum(tile + 1, columns // LANES - 1) * LANES, LANES)
    keep_before = (tile > 0).astype(jnp.float32)
    keep_after = (tile + 1 < columns // LANES).astype(jnp.float32)
    lane = lax.broadcasted_iota(jnp.int32, (rows, LANES), 1)

    def fill(ref, j, source):
        mid = source[j, :, pl.ds(start, LANES)].astype(jnp.float32)
        left = source[j, :, pl.ds(before, LANES)].astype(jnp.float32) * keep_before
        right = source[j, :, pl.ds(after, LANES)].astype(jnp.float32) * keep_after
        west = jnp.where(lane == 0, pltpu.roll(left, 1, 1), pltpu.roll(mid, 1, 1))
        east = jnp.where(
            lane == LANES - 1, pltpu.roll(right, LANES - 1, 1), pltpu.roll(mid, LANES - 1, 1)
        )
        vals[ref, pl.ds(PAD, rows), :] = mid * 0.5
        vals[ref, pl.ds(PAD - 1, 1), :] = low[ref, :, pl.ds(start, LANES)] * 0.5
        vals[ref, pl.ds(PAD + rows, 1), :] = high[ref, :, pl.ds(start, LANES)] * 0.5
        across = vals[ref, pl.ds(PAD + 1, rows), :] - vals[ref, pl.ds(PAD - 1, rows), :]
        along = (east - west) * 0.5
        grads[ref] = across * across + along * along

    def body(j, carry):
        fill(j, j, vol)
        return carry

    lax.fori_loop(0, slices, body, 0, unroll=4)
    fill(slices, 0, nxt)


def march_tile(samples, table, vals, grads, slices, rows, bins):
    count = jnp.full((rows, LANES), samples.astype(jnp.float32))
    inverse = 1.0 / count
    extinct = (-slices * math.log2(math.e)) * inverse
    half = 0.5 * (bins - 1)
    rows_of = [jnp.broadcast_to(table[c : c + 1, :], (rows, LANES)) for c in range(8)]

    def group(number, carry):
        red, green, blue, remain = carry
        for inner in range(GROUP):
            k = number * GROUP + inner
            valid = k < samples
            travel = jnp.minimum(k + 1, samples) * slices
            base = jnp.minimum(lax.div(travel, samples), slices - 1)
            part = (travel - base * samples).astype(jnp.float32) * inverse
            v0 = vals[base, pl.ds(PAD, rows), :]
            v1 = vals[base + 1, pl.ds(PAD, rows), :]
            q0 = grads[base]
            q1 = grads[base + 1]
            level = half * jnp.tanh(v0 + part * (v1 - v0)) + half
            shift = q0 + part * (q1 - q0)
            index = level.astype(jnp.int32)
            frac = level - index.astype(jnp.float32)
            upper = rounded(frac)
            lower = rounded(1.0 - frac)
            looked = [
                lower * gather_lanes(rows_of[c], index) + upper * gather_lanes(rows_of[c + 4], index)
                for c in range(4)
            ]
            shade = 1.0 - 0.6 / (1.0 + shift)
            rate = jnp.where(valid, 1.0, 0.0) * extinct
            left = remain * jnp.exp2(looked[3] * rate)
            weight = (remain - left) * shade
            red = red + weight * looked[0]
            green = green + weight * looked[1]
            blue = blue + weight * looked[2]
            remain = left
        return red, green, blue, remain

    zero = jnp.zeros((rows, LANES), jnp.float32)
    groups = lax.div(samples + (GROUP - 1), GROUP)
    return lax.fori_loop(0, groups, group, (zero, zero, zero, zero + 1.0))


def march_kernel(bins, listed, counts, vol, nxt, low, high, table, out, vals, grads):
    slices, rows, columns = vol.shape
    out[...] = jnp.zeros_like(out)

    def per_slot(slot, carry):
        tile = listed[slot]

        @pl.when(tile >= 0)
        def _():
            prepare_tile(tile, vol, nxt, low, high, vals, grads)
            red, green, blue, remain = march_tile(
                counts[tile], table, vals, grads, slices, rows, bins
            )
            where = pl.ds(pl.multiple_of(tile * LANES, LANES), LANES)
            out[0, :, where] = red
            out[1, :, where] = green
            out[2, :, where] = blue
            out[3, :, where] = 1.0 - remain

        return carry

    lax.fori_loop(0, columns // LANES, per_slot, 0)


def shards(volume, occupied, sample_counts, depth_order, colors, density):
    slices, rows, columns = volume.shape
    bins = colors.shape[1]
    bricks, groups = lax.axis_size("view"), lax.axis_size("img")
    table = jnp.concatenate([colors, density[None, :]], axis=0).astype(jnp.float32)
    table = jnp.concatenate([table, jnp.pad(table[:, 1:], ((0, 0), (0, 1)))], axis=0)

    def moved(value, view_step, img_step):
        pairs = []
        for b in range(bricks):
            for g in range(groups):
                tb, tg = b + view_step, g + img_step
                if 0 <= tb < bricks and 0 <= tg < groups:
                    pairs.append((b * groups + g, tb * groups + tg))
        return lax.ppermute(value, ("view", "img"), pairs)

    first, last = volume[:, 0, :], volume[:, rows - 1, :]
    nxt = moved(volume[0:1], -1, 0)
    low = jnp.concatenate([moved(last, 0, 1), moved(last[0:1], -1, 1)], axis=0)
    high = jnp.concatenate([moved(first, 0, -1), moved(first[0:1], -1, -1)], axis=0)
    vmem = pl.BlockSpec(memory_space=pltpu.VMEM)
    smem = pl.BlockSpec(memory_space=pltpu.SMEM)
    partial_value = pl.pallas_call(
        functools.partial(march_kernel, bins),
        out_shape=jax.ShapeDtypeStruct((4, rows, columns), jnp.float32),
        in_specs=[smem, smem, vmem, vmem, vmem, vmem, vmem],
        out_specs=vmem,
        scratch_shapes=[
            pltpu.VMEM((slices + 1, rows + 2 * PAD, LANES), jnp.float32),
            pltpu.VMEM((slices + 1, rows, LANES), jnp.float32),
        ],
        name="march",
    )(
        occupied[0, 0],
        sample_counts[0, 0],
        volume,
        nxt,
        low.astype(jnp.float32)[:, None],
        high.astype(jnp.float32)[:, None],
        table,
    )
    received = lax.all_to_all(partial_value[None], "view", split_axis=3, concat_axis=0, tiled=True)
    image = jnp.zeros(received.shape[1:], jnp.float32)
    remain = jnp.ones(received.shape[2:], jnp.float32)
    for position in range(bricks):
        chosen = lax.dynamic_index_in_dim(received, depth_order[position], 0, keepdims=False)
        image = image + remain[None] * chosen
        remain = remain * (1.0 - chosen[3])
    return image


def solution(mesh):
    return jax.shard_map(
        shards,
        mesh=mesh,
        in_specs=(
            P("view", "img", None),
            P("view", "img", None),
            P("view", "img", None),
            P(),
            P(),
            P(),
        ),
        out_specs=P(None, "img", "view"),
        check_vma=False,
    )
```

```python
import functools
import math

import jax
import jax.numpy as jnp
from jax import lax
from jax.experimental import pallas as pl
from jax.experimental.pallas import tpu as pltpu
from jax.sharding import PartitionSpec as P

LANES = 128
GROUP = 4
PAD = 8
LIMIT = 32767


def gather_lanes(row, index):
    return jnp.take_along_axis(row, index, axis=1, mode="promise_in_bounds")


def rounded(value):
    return value.astype(jnp.bfloat16).astype(jnp.float32)


def prepare_tile(tile, vol, nxt, low, high, vals, grads):
    slices, rows, columns = vol.shape
    start = pl.multiple_of(tile * LANES, LANES)
    before = pl.multiple_of(jnp.maximum(tile - 1, 0) * LANES, LANES)
    after = pl.multiple_of(jnp.minimum(tile + 1, columns // LANES - 1) * LANES, LANES)
    keep_before = (tile > 0).astype(jnp.float32)
    keep_after = (tile + 1 < columns // LANES).astype(jnp.float32)
    lane = lax.broadcasted_iota(jnp.int32, (rows, LANES), 1)

    def fill(ref, j, source):
        mid = source[j, :, pl.ds(start, LANES)].astype(jnp.float32)
        left = source[j, :, pl.ds(before, LANES)].astype(jnp.float32) * keep_before
        right = source[j, :, pl.ds(after, LANES)].astype(jnp.float32) * keep_after
        west = jnp.where(lane == 0, pltpu.roll(left, 1, 1), pltpu.roll(mid, 1, 1))
        east = jnp.where(
            lane == LANES - 1, pltpu.roll(right, LANES - 1, 1), pltpu.roll(mid, LANES - 1, 1)
        )
        vals[ref, pl.ds(PAD, rows), :] = mid * 0.5
        vals[ref, pl.ds(PAD - 1, 1), :] = low[ref, :, pl.ds(start, LANES)] * 0.5
        vals[ref, pl.ds(PAD + rows, 1), :] = high[ref, :, pl.ds(start, LANES)] * 0.5
        across = vals[ref, pl.ds(PAD + 1, rows), :] - vals[ref, pl.ds(PAD - 1, rows), :]
        along = (east - west) * 0.5
        grads[ref] = across * across + along * along

    def body(j, carry):
        fill(j, j, vol)
        return carry

    lax.fori_loop(0, slices, body, 0, unroll=4)
    fill(slices, 0, nxt)


def march_tile(samples, table, vals, grads, slices, rows, bins):
    count = jnp.full((rows, LANES), samples.astype(jnp.float32))
    inverse = 1.0 / count
    extinct = (-slices * math.log2(math.e)) * inverse
    half = 0.5 * (bins - 1)
    rows_of = [jnp.broadcast_to(table[c : c + 1, :], (rows, LANES)) for c in range(8)]

    def group(number, carry):
        red, green, blue, remain = carry
        for inner in range(GROUP):
            k = number * GROUP + inner
            valid = k < samples
            travel = jnp.minimum(k + 1, samples) * slices
            base = jnp.minimum(lax.div(travel, samples), slices - 1)
            part = (travel - base * samples).astype(jnp.float32) * inverse
            v0 = vals[base, pl.ds(PAD, rows), :]
            v1 = vals[base + 1, pl.ds(PAD, rows), :]
            q0 = grads[base]
            q1 = grads[base + 1]
            level = half * jnp.tanh(v0 + part * (v1 - v0)) + half
            shift = q0 + part * (q1 - q0)
            index = level.astype(jnp.int32)
            frac = level - index.astype(jnp.float32)
            upper = rounded(frac)
            lower = rounded(1.0 - frac)
            looked = [
                lower * gather_lanes(rows_of[c], index) + upper * gather_lanes(rows_of[c + 4], index)
                for c in range(4)
            ]
            shade = 1.0 - 0.6 / (1.0 + shift)
            rate = jnp.where(valid, 1.0, 0.0) * extinct
            left = remain * jnp.exp2(looked[3] * rate)
            weight = (remain - left) * shade
            red = red + weight * looked[0]
            green = green + weight * looked[1]
            blue = blue + weight * looked[2]
            remain = left
        return red, green, blue, remain

    zero = jnp.zeros((rows, LANES), jnp.float32)
    groups = lax.div(samples + (GROUP - 1), GROUP)
    return lax.fori_loop(0, groups, group, (zero, zero, zero, zero + 1.0))


def channel_bounds(table, slices):
    largest = jnp.max(table[0:4, :], axis=1, keepdims=True)
    cover = 1.0 - jnp.exp2((-1.01 * math.log2(math.e) * slices) * largest[3:4])
    return [1.01 * cover * (largest[c : c + 1] if c < 3 else 1.0) for c in range(4)]


def march_kernel(bins, listed, counts, vol, nxt, low, high, table, out, vals, grads):
    slices, rows, columns = vol.shape
    per = out.shape[3] // LANES
    out[...] = jnp.full(out.shape, -LIMIT, jnp.int16)
    scales = [2.0 * LIMIT / bound for bound in channel_bounds(table, slices)]

    def per_slot(slot, carry):
        tile = listed[slot]

        @pl.when(tile >= 0)
        def _():
            prepare_tile(tile, vol, nxt, low, high, vals, grads)
            red, green, blue, remain = march_tile(
                counts[tile], table, vals, grads, slices, rows, bins
            )
            owner = lax.div(tile, per)
            where = pl.ds(pl.multiple_of((tile - owner * per) * LANES, LANES), LANES)
            for c, value in enumerate((red, green, blue, 1.0 - remain)):
                code = (value * scales[c] + 0.5).astype(jnp.int32) - LIMIT
                out[owner, c, :, where] = code.astype(jnp.int16)

        return carry

    lax.fori_loop(0, columns // LANES, per_slot, 0)


def halo_kernel(bricks, groups, top, first, last, nxt, low, high, send, recv):
    b, g = lax.axis_index("view"), lax.axis_index("img")
    slices = first.shape[0]
    barrier = pltpu.get_barrier_semaphore()
    steps = [(0, 1), (0, -1), (-1, 0), (-1, 1), (-1, -1)]

    def exists(vb, vg):
        return jnp.logical_and(
            jnp.logical_and(b + vb >= 0, b + vb < bricks),
            jnp.logical_and(g + vg >= 0, g + vg < groups),
        )

    met = jnp.int32(0)
    for vb, vg in steps + [(1, 0), (1, 1), (1, -1)]:
        here = exists(vb, vg)

        @pl.when(here)
        def _(vb=vb, vg=vg):
            pl.semaphore_signal(
                barrier, inc=1, device_id=(b + vb, g + vg), device_id_type=pl.DeviceIdType.MESH
            )

        met = met + here.astype(jnp.int32)
    pl.semaphore_wait(barrier, met)
    main, extra = pl.ds(0, slices), pl.ds(slices, 1)
    plan = [
        (last, low.at[main]),
        (first, high.at[main]),
        (top, nxt),
        (last.at[pl.ds(0, 1)], low.at[extra]),
        (first.at[pl.ds(0, 1)], high.at[extra]),
    ]

    def copy(i):
        (vb, vg), (source, target) = steps[i], plan[i]
        return pltpu.make_async_remote_copy(
            src_ref=source,
            dst_ref=target,
            send_sem=send.at[i],
            recv_sem=recv.at[i],
            device_id=(b + vb, g + vg),
            device_id_type=pl.DeviceIdType.MESH,
        )

    for i, (vb, vg) in enumerate(steps):

        @pl.when(exists(vb, vg))
        def _(i=i):
            copy(i).start()

        @pl.when(jnp.logical_not(exists(-vb, -vg)))
        def _(i=i):
            plan[i][1][...] = jnp.zeros(plan[i][1].shape, plan[i][1].dtype)

    for i, (vb, vg) in enumerate(steps):

        @pl.when(exists(vb, vg))
        def _(i=i):
            copy(i).wait_send()

        @pl.when(exists(-vb, -vg))
        def _(i=i):
            copy(i).wait_recv()


def blend_kernel(bricks, slices, order, mine, table, out, held, local, send, recv):
    b, g = lax.axis_index("view"), lax.axis_index("img")
    barrier = pltpu.get_barrier_semaphore()
    for step in range(1, bricks):
        pl.semaphore_signal(
            barrier,
            inc=1,
            device_id=(lax.rem(b + step, bricks), g),
            device_id_type=pl.DeviceIdType.MESH,
        )
    kept = pltpu.make_async_copy(mine.at[b], held.at[b], local)
    kept.start()
    pl.semaphore_wait(barrier, bricks - 1)
    copies = []
    for step in sorted(range(1, bricks), key=lambda r: (abs(r - bricks // 2), r)):
        peer = lax.rem(b + step, bricks)
        copies.append(
            pltpu.make_async_remote_copy(
                src_ref=mine.at[peer],
                dst_ref=held.at[b],
                send_sem=send.at[step],
                recv_sem=recv.at[step],
                device_id=(peer, g),
                device_id_type=pl.DeviceIdType.MESH,
            )
        )
        copies[-1].start()
    bounds = channel_bounds(table, slices)
    rows, narrow = out.shape[1:]
    units = [jnp.broadcast_to(bound / (2.0 * LIMIT), (rows, narrow)) for bound in bounds]
    kept.wait()
    for copy in copies:
        copy.wait()

    image = [jnp.zeros((rows, narrow), jnp.float32) for _ in range(4)]
    remain = jnp.ones((rows, narrow), jnp.float32)
    for position in range(bricks):
        chosen = order[position]
        value = [
            (held[chosen, c].astype(jnp.float32) + float(LIMIT)) * units[c] for c in range(4)
        ]
        image = [image[c] + remain * value[c] for c in range(4)]
        remain = remain * (1.0 - value[3])
    for c in range(4):
        out[c] = image[c]


def shards(volume, occupied, sample_counts, depth_order, colors, density):
    slices, rows, columns = volume.shape
    bins = colors.shape[1]
    bricks, groups = lax.axis_size("view"), lax.axis_size("img")
    narrow = columns // bricks
    table = jnp.concatenate([colors, density[None, :]], axis=0).astype(jnp.float32)
    table = jnp.concatenate([table, jnp.pad(table[:, 1:], ((0, 0), (0, 1)))], axis=0)
    vmem = pl.BlockSpec(memory_space=pltpu.VMEM)
    smem = pl.BlockSpec(memory_space=pltpu.SMEM)
    first = volume[:, 0:1, :].astype(jnp.float32)
    last = volume[:, rows - 1 : rows, :].astype(jnp.float32)
    nxt, low, high = pl.pallas_call(
        functools.partial(halo_kernel, bricks, groups),
        out_shape=(
            jax.ShapeDtypeStruct((1, rows, columns), volume.dtype),
            jax.ShapeDtypeStruct((slices + 1, 1, columns), jnp.float32),
            jax.ShapeDtypeStruct((slices + 1, 1, columns), jnp.float32),
        ),
        in_specs=[vmem] * 3,
        out_specs=(vmem,) * 3,
        scratch_shapes=[pltpu.SemaphoreType.DMA((5,)), pltpu.SemaphoreType.DMA((5,))],
        compiler_params=pltpu.CompilerParams(collective_id=0, has_side_effects=True),
        name="halo",
    )(volume[0:1], first, last)
    coded = pl.pallas_call(
        functools.partial(march_kernel, bins),
        out_shape=jax.ShapeDtypeStruct((bricks, 4, rows, narrow), jnp.int16),
        in_specs=[smem, smem, vmem, vmem, vmem, vmem, vmem],
        out_specs=vmem,
        scratch_shapes=[
            pltpu.VMEM((slices + 1, rows + 2 * PAD, LANES), jnp.float32),
            pltpu.VMEM((slices + 1, rows, LANES), jnp.float32),
        ],
        name="march",
    )(occupied[0, 0], sample_counts[0, 0], volume, nxt, low, high, table)
    return pl.pallas_call(
        functools.partial(blend_kernel, bricks, slices),
        out_shape=jax.ShapeDtypeStruct((4, rows, narrow), jnp.float32),
        in_specs=[smem, vmem, vmem],
        out_specs=vmem,
        scratch_shapes=[
            pltpu.VMEM((bricks, 4, rows, narrow), jnp.int16),
            pltpu.SemaphoreType.DMA,
            pltpu.SemaphoreType.DMA((bricks,)),
            pltpu.SemaphoreType.DMA((bricks,)),
        ],
        compiler_params=pltpu.CompilerParams(collective_id=1, has_side_effects=True),
        name="blend",
    )(depth_order, coded, table)


def solution(mesh):
    return jax.shard_map(
        shards,
        mesh=mesh,
        in_specs=(
            P("view", "img", None),
            P("view", "img", None),
            P("view", "img", None),
            P(),
            P(),
            P(),
        ),
        out_specs=P(None, "img", "view"),
        check_vma=False,
    )
```

```python
import functools
import math

import jax
import jax.numpy as jnp
from jax import lax
from jax.experimental import pallas as pl
from jax.experimental.pallas import tpu as pltpu
from jax.sharding import PartitionSpec as P

LANES = 128
GROUP = 8
PAD = 8
STRIP = 8
LIMIT = 32767
LEVELS = (4096.0, 4096.0, 4096.0, 65536.0)
SPAN_BITS = 13
SPAN = 1 << SPAN_BITS
PACKED = (0, 1, 2, 3)


LANE_GATHER = lax.GatherDimensionNumbers(
    offset_dims=(),
    collapsed_slice_dims=(1,),
    start_index_map=(1,),
    operand_batching_dims=(0,),
    start_indices_batching_dims=(0,),
)


def gather_lanes(row, index):
    return lax.gather(
        row, index[..., None], LANE_GATHER, (1, 1), mode=lax.GatherScatterMode.PROMISE_IN_BOUNDS
    )


def rounded(value):
    return value.astype(jnp.bfloat16).astype(jnp.float32)


def prepare_tile(tile, vol, nxt, low, high, vals, grads):
    slices, rows, columns = vol.shape
    start = pl.multiple_of(tile * LANES, LANES)
    before = pl.multiple_of(jnp.maximum(tile - 1, 0) * LANES, LANES)
    after = pl.multiple_of(jnp.minimum(tile + 1, columns // LANES - 1) * LANES, LANES)
    keep_before = (tile > 0).astype(jnp.float32)
    keep_after = (tile + 1 < columns // LANES).astype(jnp.float32)
    lane = lax.broadcasted_iota(jnp.int32, (rows, LANES), 1)

    def fill(ref, j, source):
        mid = source[j, :, pl.ds(start, LANES)].astype(jnp.float32)
        left = source[j, :, pl.ds(before, LANES)].astype(jnp.float32) * keep_before
        right = source[j, :, pl.ds(after, LANES)].astype(jnp.float32) * keep_after
        west = jnp.where(lane == 0, pltpu.roll(left, 1, 1), pltpu.roll(mid, 1, 1))
        east = jnp.where(
            lane == LANES - 1, pltpu.roll(right, LANES - 1, 1), pltpu.roll(mid, LANES - 1, 1)
        )
        vals[ref, pl.ds(PAD, rows), :] = mid * 0.5
        vals[ref, pl.ds(PAD - 1, 1), :] = low[ref, :, pl.ds(start, LANES)] * 0.5
        vals[ref, pl.ds(PAD + rows, 1), :] = high[ref, :, pl.ds(start, LANES)] * 0.5
        across = vals[ref, pl.ds(PAD + 1, rows), :] - vals[ref, pl.ds(PAD - 1, rows), :]
        along = (east - west) * 0.5
        grads[ref] = (across * across + along * along) * (1.0 / 0.6) + (1.0 / 0.6)

    def body(j, carry):
        fill(j, j, vol)
        return carry

    lax.fori_loop(0, slices, body, 0, unroll=4)
    fill(slices, 0, nxt)


def march_tile(samples, table, vals, grads, slices, rows, bins):
    inverse = 1.0 / jnp.full((STRIP, LANES), samples.astype(jnp.float32))
    unit = 1.0 / LEVELS[3] if 3 in PACKED else 1.0
    extinct = (-slices * math.log2(math.e) * unit) * inverse
    half = 0.5 * (bins - 1)
    rows_of = [jnp.broadcast_to(table[c : c + 1, :], (STRIP, LANES)) for c in range(8)]
    pairs = {}
    for c in PACKED:
        whole = (rows_of[c] * LEVELS[c]).astype(jnp.int32) * SPAN
        pairs[c] = whole + (rows_of[c + 4] * LEVELS[c]).astype(jnp.int32)
    strips = rows // STRIP

    def group(number, carry):
        carry = list(carry)
        for inner in range(GROUP):
            k = number * GROUP + inner
            valid = k < samples
            travel = jnp.minimum(k + 1, samples) * slices
            base = jnp.minimum(lax.div(travel, samples), slices - 1)
            part = (travel - base * samples).astype(jnp.float32) * inverse
            rate = jnp.where(valid, 1.0, 0.0) * extinct
            for strip in range(strips):
                red, green, blue, remain = carry[4 * strip : 4 * strip + 4]
                v0 = vals[base, pl.ds(PAD + strip * STRIP, STRIP), :]
                v1 = vals[base + 1, pl.ds(PAD + strip * STRIP, STRIP), :]
                q0 = grads[base, pl.ds(strip * STRIP, STRIP), :]
                q1 = grads[base + 1, pl.ds(strip * STRIP, STRIP), :]
                level = half * jnp.tanh(v0 + part * (v1 - v0)) + half
                shift = q0 + part * (q1 - q0)
                index = level.astype(jnp.int32)
                frac = level - index.astype(jnp.float32)
                upper = rounded(frac)
                lower = rounded(1.0 - frac)
                found = [None] * 8
                for c in range(4):
                    if c in PACKED:
                        both = gather_lanes(pairs[c], index)
                        found[c] = lax.shift_right_logical(both, SPAN_BITS).astype(jnp.float32)
                        found[c + 4] = lax.bitwise_and(both, SPAN - 1).astype(jnp.float32)
                    else:
                        found[c] = gather_lanes(rows_of[c], index)
                        found[c + 4] = gather_lanes(rows_of[c + 4], index)
                sigma = lower * found[3] + upper * found[7]
                left = remain * jnp.exp2(sigma * rate)
                weight = (remain - left) * (1.0 - 1.0 / shift)
                near = weight * lower
                far = weight * upper
                carry[4 * strip : 4 * strip + 4] = [
                    red + near * found[0] + far * found[4],
                    green + near * found[1] + far * found[5],
                    blue + near * found[2] + far * found[6],
                    left,
                ]
        return tuple(carry)

    zero = jnp.zeros((STRIP, LANES), jnp.float32)
    groups = lax.div(samples + (GROUP - 1), GROUP)
    done = lax.fori_loop(0, groups, group, (zero, zero, zero, zero + 1.0) * strips)
    units = [1.0 / LEVELS[c] if c in PACKED and c < 3 else 1.0 for c in range(4)]
    return [jnp.concatenate(done[c::4], axis=0) * units[c] for c in range(4)]


def channel_bounds(table, slices):
    largest = jnp.max(table[0:4, :], axis=1, keepdims=True)
    cover = 1.0 - jnp.exp2((-1.01 * math.log2(math.e) * slices) * largest[3:4])
    return [1.01 * cover * (largest[c : c + 1] if c < 3 else 1.0) for c in range(4)]


def march_kernel(bins, listed, counts, vol, nxt, low, high, table, out, vals, grads):
    slices, rows, columns = vol.shape
    per = out.shape[3] // LANES
    out[...] = jnp.full(out.shape, -LIMIT, jnp.int16)
    scales = [2.0 * LIMIT / bound for bound in channel_bounds(table, slices)]

    def per_slot(slot, carry):
        tile = listed[slot]

        @pl.when(tile >= 0)
        def _():
            prepare_tile(tile, vol, nxt, low, high, vals, grads)
            red, green, blue, remain = march_tile(
                counts[tile], table, vals, grads, slices, rows, bins
            )
            owner = lax.div(tile, per)
            where = pl.ds(pl.multiple_of((tile - owner * per) * LANES, LANES), LANES)
            for c, value in enumerate((red, green, blue, 1.0 - remain)):
                code = (value * scales[c] + 0.5).astype(jnp.int32) - LIMIT
                out[owner, c, :, where] = code.astype(jnp.int16)

        return carry

    lax.fori_loop(0, columns // LANES, per_slot, 0)


def halo_kernel(bricks, groups, top, first, last, nxt, low, high, send, recv):
    b, g = lax.axis_index("view"), lax.axis_index("img")
    slices = first.shape[0]
    barrier = pltpu.get_barrier_semaphore()
    steps = [(0, 1), (0, -1), (-1, 0), (-1, 1), (-1, -1)]

    def exists(vb, vg):
        return jnp.logical_and(
            jnp.logical_and(b + vb >= 0, b + vb < bricks),
            jnp.logical_and(g + vg >= 0, g + vg < groups),
        )

    met = jnp.int32(0)
    for vb, vg in steps + [(1, 0), (1, 1), (1, -1)]:
        here = exists(vb, vg)

        @pl.when(here)
        def _(vb=vb, vg=vg):
            pl.semaphore_signal(
                barrier, inc=1, device_id=(b + vb, g + vg), device_id_type=pl.DeviceIdType.MESH
            )

        met = met + here.astype(jnp.int32)
    pl.semaphore_wait(barrier, met)
    main, extra = pl.ds(0, slices), pl.ds(slices, 1)
    plan = [
        (last, low.at[main]),
        (first, high.at[main]),
        (top, nxt),
        (last.at[pl.ds(0, 1)], low.at[extra]),
        (first.at[pl.ds(0, 1)], high.at[extra]),
    ]

    def copy(i):
        (vb, vg), (source, target) = steps[i], plan[i]
        return pltpu.make_async_remote_copy(
            src_ref=source,
            dst_ref=target,
            send_sem=send.at[i],
            recv_sem=recv.at[i],
            device_id=(b + vb, g + vg),
            device_id_type=pl.DeviceIdType.MESH,
        )

    for i, (vb, vg) in enumerate(steps):

        @pl.when(exists(vb, vg))
        def _(i=i):
            copy(i).start()

        @pl.when(jnp.logical_not(exists(-vb, -vg)))
        def _(i=i):
            plan[i][1][...] = jnp.zeros(plan[i][1].shape, plan[i][1].dtype)

    for i, (vb, vg) in enumerate(steps):

        @pl.when(exists(vb, vg))
        def _(i=i):
            copy(i).wait_send()

        @pl.when(exists(-vb, -vg))
        def _(i=i):
            copy(i).wait_recv()


def blend_kernel(bricks, slices, order, mine, table, out, held, local, send, recv):
    b, g = lax.axis_index("view"), lax.axis_index("img")
    barrier = pltpu.get_barrier_semaphore()
    for step in range(1, bricks):
        pl.semaphore_signal(
            barrier,
            inc=1,
            device_id=(lax.rem(b + step, bricks), g),
            device_id_type=pl.DeviceIdType.MESH,
        )
    kept = pltpu.make_async_copy(mine.at[b], held.at[b], local)
    kept.start()
    pl.semaphore_wait(barrier, bricks - 1)
    copies = []
    for step in sorted(range(1, bricks), key=lambda r: (abs(r - bricks // 2), r)):
        peer = lax.rem(b + step, bricks)
        copies.append(
            pltpu.make_async_remote_copy(
                src_ref=mine.at[peer],
                dst_ref=held.at[b],
                send_sem=send.at[step],
                recv_sem=recv.at[step],
                device_id=(peer, g),
                device_id_type=pl.DeviceIdType.MESH,
            )
        )
        copies[-1].start()
    bounds = channel_bounds(table, slices)
    rows, narrow = out.shape[1:]
    units = [jnp.broadcast_to(bound / (2.0 * LIMIT), (rows, narrow)) for bound in bounds]
    kept.wait()
    for copy in copies:
        copy.wait()

    image = [jnp.zeros((rows, narrow), jnp.float32) for _ in range(4)]
    remain = jnp.ones((rows, narrow), jnp.float32)
    for position in range(bricks):
        chosen = order[position]
        value = [
            (held[chosen, c].astype(jnp.float32) + float(LIMIT)) * units[c] for c in range(4)
        ]
        image = [image[c] + remain * value[c] for c in range(4)]
        remain = remain * (1.0 - value[3])
    for c in range(4):
        out[c] = image[c]


def shards(volume, occupied, sample_counts, depth_order, colors, density):
    slices, rows, columns = volume.shape
    bins = colors.shape[1]
    bricks, groups = lax.axis_size("view"), lax.axis_size("img")
    narrow = columns // bricks
    table = jnp.concatenate([colors, density[None, :]], axis=0).astype(jnp.float32)
    table = jnp.concatenate([table, jnp.pad(table[:, 1:], ((0, 0), (0, 1)))], axis=0)
    vmem = pl.BlockSpec(memory_space=pltpu.VMEM)
    smem = pl.BlockSpec(memory_space=pltpu.SMEM)
    first = volume[:, 0:1, :].astype(jnp.float32)
    last = volume[:, rows - 1 : rows, :].astype(jnp.float32)
    nxt, low, high = pl.pallas_call(
        functools.partial(halo_kernel, bricks, groups),
        out_shape=(
            jax.ShapeDtypeStruct((1, rows, columns), volume.dtype),
            jax.ShapeDtypeStruct((slices + 1, 1, columns), jnp.float32),
            jax.ShapeDtypeStruct((slices + 1, 1, columns), jnp.float32),
        ),
        in_specs=[vmem] * 3,
        out_specs=(vmem,) * 3,
        scratch_shapes=[pltpu.SemaphoreType.DMA((5,)), pltpu.SemaphoreType.DMA((5,))],
        compiler_params=pltpu.CompilerParams(collective_id=0, has_side_effects=True),
        name="halo",
    )(volume[0:1], first, last)
    coded = pl.pallas_call(
        functools.partial(march_kernel, bins),
        out_shape=jax.ShapeDtypeStruct((bricks, 4, rows, narrow), jnp.int16),
        in_specs=[smem, smem, vmem, vmem, vmem, vmem, vmem],
        out_specs=vmem,
        scratch_shapes=[
            pltpu.VMEM((slices + 1, rows + 2 * PAD, LANES), jnp.float32),
            pltpu.VMEM((slices + 1, rows, LANES), jnp.float32),
        ],
        name="march",
    )(occupied[0, 0], sample_counts[0, 0], volume, nxt, low, high, table)
    return pl.pallas_call(
        functools.partial(blend_kernel, bricks, slices),
        out_shape=jax.ShapeDtypeStruct((4, rows, narrow), jnp.float32),
        in_specs=[smem, vmem, vmem],
        out_specs=vmem,
        scratch_shapes=[
            pltpu.VMEM((bricks, 4, rows, narrow), jnp.int16),
            pltpu.SemaphoreType.DMA,
            pltpu.SemaphoreType.DMA((bricks,)),
            pltpu.SemaphoreType.DMA((bricks,)),
        ],
        compiler_params=pltpu.CompilerParams(collective_id=1, has_side_effects=True),
        name="blend",
    )(depth_order, coded, table)


def solution(mesh):
    return jax.shard_map(
        shards,
        mesh=mesh,
        in_specs=(
            P("view", "img", None),
            P("view", "img", None),
            P("view", "img", None),
            P(),
            P(),
            P(),
        ),
        out_specs=P(None, "img", "view"),
        check_vma=False,
    )
```

```python
import functools
import math

import jax
import jax.numpy as jnp
from jax import lax
from jax.experimental import pallas as pl
from jax.experimental.pallas import tpu as pltpu
from jax.sharding import PartitionSpec as P

LANES = 128
GROUP = 8
PAD = 8
STRIP = 8
LIMIT = 32767
LEVELS = (4096.0, 4096.0, 4096.0, 65536.0)
SPAN_BITS = 13
SPAN = 1 << SPAN_BITS
CHUNK = 4


LANE_GATHER = lax.GatherDimensionNumbers(
    offset_dims=(),
    collapsed_slice_dims=(1,),
    start_index_map=(1,),
    operand_batching_dims=(0,),
    start_indices_batching_dims=(0,),
)


def gather_lanes(row, index):
    return lax.gather(
        row, index[..., None], LANE_GATHER, (1, 1), mode=lax.GatherScatterMode.PROMISE_IN_BOUNDS
    )


def rounded(value):
    return value.astype(jnp.bfloat16).astype(jnp.float32)


def prepare_tile(tile, vol, nxt, low, high, vals, grads):
    slices, rows, columns = vol.shape
    last = columns // LANES - 1
    starts = [
        pl.multiple_of(jnp.maximum(tile - 1, 0) * LANES, LANES),
        pl.multiple_of(tile * LANES, LANES),
        pl.multiple_of(jnp.minimum(tile + 1, last) * LANES, LANES),
    ]
    source = lax.broadcasted_iota(jnp.int32, (3 * LANES, LANES), 0) - LANES
    target = lax.broadcasted_iota(jnp.int32, (3 * LANES, LANES), 1)
    inside = jnp.logical_and(
        jnp.logical_or(source >= 0, tile > 0), jnp.logical_or(source < LANES, tile < last)
    )
    sign = jnp.where(source == target + 1, 0.5, jnp.where(source == target - 1, -0.5, 0.0))
    weights = jnp.where(inside, sign, 0.0).astype(jnp.bfloat16)
    here = pl.ds(starts[1], LANES)

    def fill(first, count, ref, at):
        blocks = [
            ref[at : at + count, :, pl.ds(start, LANES)].reshape(count * rows, LANES)
            for start in starts
        ]
        along = jnp.dot(
            jnp.concatenate(blocks, axis=1), weights, preferred_element_type=jnp.float32
        ).reshape(count, rows, LANES)
        mid = blocks[1].astype(jnp.float32).reshape(count, rows, LANES)
        for j in range(count):
            z = first + j
            vals[z, PAD : PAD + rows, :] = mid[j] * 0.5
            vals[z, PAD - 1 : PAD, :] = low[z, :, here] * 0.5
            vals[z, PAD + rows : PAD + rows + 1, :] = high[z, :, here] * 0.5
        for j in range(count):
            z = first + j
            across = vals[z, PAD + 1 : PAD + 1 + rows, :] - vals[z, PAD - 1 : PAD - 1 + rows, :]
            grads[z] = (across * across + along[j] * along[j]) * (1.0 / 0.6) + (1.0 / 0.6)

    for first in range(0, slices, CHUNK):
        fill(first, CHUNK, vol, first)
    fill(slices, 1, nxt, 0)


def packed_table(colors, density):
    entries = [colors[c : c + 1, :] for c in range(3)] + [density]
    lane = lax.broadcasted_iota(jnp.int32, (STRIP, LANES), 1)
    pairs = []
    for entry, level in zip(entries, LEVELS):
        whole = (jnp.broadcast_to(entry, (STRIP, LANES)) * level).astype(jnp.int32)
        after = jnp.where(lane == LANES - 1, 0, pltpu.roll(whole, LANES - 1, 1))
        pairs.append(whole * SPAN + after)
    return pairs


def march_tile(samples, pairs, vals, grads, slices, rows, bins):
    inverse = 1.0 / jnp.full((STRIP, LANES), samples.astype(jnp.float32))
    extinct = (-slices * math.log2(math.e) / LEVELS[3]) * inverse
    half = 0.5 * (bins - 1)
    strips = rows // STRIP

    def group(number, carry):
        carry = list(carry)
        for inner in range(GROUP):
            k = number * GROUP + inner
            valid = k < samples
            travel = jnp.minimum(k + 1, samples) * slices
            base = jnp.minimum(lax.div(travel, samples), slices - 1)
            part = (travel - base * samples).astype(jnp.float32) * inverse
            rate = jnp.where(valid, 1.0, 0.0) * extinct
            for strip in range(strips):
                red, green, blue, remain = carry[4 * strip : 4 * strip + 4]
                v0 = vals[base, pl.ds(PAD + strip * STRIP, STRIP), :]
                v1 = vals[base + 1, pl.ds(PAD + strip * STRIP, STRIP), :]
                q0 = grads[base, pl.ds(strip * STRIP, STRIP), :]
                q1 = grads[base + 1, pl.ds(strip * STRIP, STRIP), :]
                level = half * jnp.tanh(v0 + part * (v1 - v0)) + half
                shift = q0 + part * (q1 - q0)
                index = level.astype(jnp.int32)
                frac = level - index.astype(jnp.float32)
                upper = rounded(frac)
                lower = rounded(1.0 - frac)
                both = [gather_lanes(pair, index) for pair in pairs]
                found = [lax.shift_right_logical(p, SPAN_BITS).astype(jnp.float32) for p in both]
                found += [lax.bitwise_and(p, SPAN - 1).astype(jnp.float32) for p in both]
                sigma = lower * found[3] + upper * found[7]
                left = remain * jnp.exp2(sigma * rate)
                weight = (remain - left) * (1.0 - 1.0 / shift)
                near = weight * lower
                far = weight * upper
                carry[4 * strip : 4 * strip + 4] = [
                    red + near * found[0] + far * found[4],
                    green + near * found[1] + far * found[5],
                    blue + near * found[2] + far * found[6],
                    left,
                ]
        return tuple(carry)

    zero = jnp.zeros((STRIP, LANES), jnp.float32)
    groups = lax.div(samples + (GROUP - 1), GROUP)
    done = lax.fori_loop(0, groups, group, (zero, zero, zero, zero + 1.0) * strips)
    units = [1.0 / level for level in LEVELS[:3]] + [1.0]
    return [jnp.concatenate(done[c::4], axis=0) * units[c] for c in range(4)]


def channel_bounds(colors, density, slices):
    cover = 1.0 - jnp.exp2(
        (-1.01 * math.log2(math.e) * slices) * jnp.max(density, axis=1, keepdims=True)
    )
    most = jnp.max(colors, axis=1, keepdims=True)
    return [1.01 * cover * (most[c : c + 1] if c < 3 else 1.0) for c in range(4)]


def march_kernel(
    bins, listed, counts, vol, nxt, low, high, colors_ref, density_ref, out, vals, grads
):
    slices, rows, columns = vol.shape
    per = out.shape[3] // LANES
    colors = colors_ref[...].astype(jnp.float32)
    density = density_ref[...].astype(jnp.float32)
    pairs = packed_table(colors, density)
    out[...] = jnp.full(out.shape, -LIMIT, jnp.int16)
    scales = [2.0 * LIMIT / bound for bound in channel_bounds(colors, density, slices)]

    def per_slot(slot, carry):
        tile = listed[slot]

        @pl.when(tile >= 0)
        def _():
            prepare_tile(tile, vol, nxt, low, high, vals, grads)
            red, green, blue, remain = march_tile(
                counts[tile], pairs, vals, grads, slices, rows, bins
            )
            owner = lax.div(tile, per)
            where = pl.ds(pl.multiple_of((tile - owner * per) * LANES, LANES), LANES)
            for c, value in enumerate((red, green, blue, 1.0 - remain)):
                code = (value * scales[c] + 0.5).astype(jnp.int32) - LIMIT
                out[owner, c, :, where] = code.astype(jnp.int16)

        return carry

    lax.fori_loop(0, columns // LANES, per_slot, 0)


def halo_kernel(bricks, groups, vol, first, last, nxt, low, high, send, recv):
    b, g = lax.axis_index("view"), lax.axis_index("img")
    slices = first.shape[0]
    barrier = pltpu.get_barrier_semaphore()
    steps = [(0, 1), (0, -1), (-1, 0), (-1, 1), (-1, -1)]

    def exists(vb, vg):
        return jnp.logical_and(
            jnp.logical_and(b + vb >= 0, b + vb < bricks),
            jnp.logical_and(g + vg >= 0, g + vg < groups),
        )

    met = jnp.int32(0)
    for vb, vg in steps + [(1, 0), (1, 1), (1, -1)]:
        here = exists(vb, vg)

        @pl.when(here)
        def _(vb=vb, vg=vg):
            pl.semaphore_signal(
                barrier, inc=1, device_id=(b + vb, g + vg), device_id_type=pl.DeviceIdType.MESH
            )

        met = met + here.astype(jnp.int32)
    pl.semaphore_wait(barrier, met)
    main, extra = pl.ds(0, slices), pl.ds(slices, 1)
    plan = [
        (last, low.at[main]),
        (first, high.at[main]),
        (vol.at[pl.ds(0, 1)], nxt),
        (last.at[pl.ds(0, 1)], low.at[extra]),
        (first.at[pl.ds(0, 1)], high.at[extra]),
    ]

    def copy(i):
        (vb, vg), (source, target) = steps[i], plan[i]
        return pltpu.make_async_remote_copy(
            src_ref=source,
            dst_ref=target,
            send_sem=send.at[i],
            recv_sem=recv.at[i],
            device_id=(b + vb, g + vg),
            device_id_type=pl.DeviceIdType.MESH,
        )

    for i, (vb, vg) in enumerate(steps):

        @pl.when(exists(vb, vg))
        def _(i=i):
            copy(i).start()

        @pl.when(jnp.logical_not(exists(-vb, -vg)))
        def _(i=i):
            plan[i][1][...] = jnp.zeros(plan[i][1].shape, plan[i][1].dtype)

    for i, (vb, vg) in enumerate(steps):

        @pl.when(exists(vb, vg))
        def _(i=i):
            copy(i).wait_send()

        @pl.when(exists(-vb, -vg))
        def _(i=i):
            copy(i).wait_recv()


def blend_kernel(bricks, slices, order, mine, colors, density, out, held, local, send, recv):
    b, g = lax.axis_index("view"), lax.axis_index("img")
    barrier = pltpu.get_barrier_semaphore()
    for step in range(1, bricks):
        pl.semaphore_signal(
            barrier,
            inc=1,
            device_id=(lax.rem(b + step, bricks), g),
            device_id_type=pl.DeviceIdType.MESH,
        )
    kept = pltpu.make_async_copy(mine.at[b], held.at[b], local)
    kept.start()
    pl.semaphore_wait(barrier, bricks - 1)
    copies = []
    for step in sorted(range(1, bricks), key=lambda r: (abs(r - bricks // 2), r)):
        peer = lax.rem(b + step, bricks)
        copies.append(
            pltpu.make_async_remote_copy(
                src_ref=mine.at[peer],
                dst_ref=held.at[b],
                send_sem=send.at[step],
                recv_sem=recv.at[step],
                device_id=(peer, g),
                device_id_type=pl.DeviceIdType.MESH,
            )
        )
        copies[-1].start()
    bounds = channel_bounds(
        colors[...].astype(jnp.float32), density[...].astype(jnp.float32), slices
    )
    rows, narrow = out.shape[1:]
    units = [jnp.broadcast_to(bound / (2.0 * LIMIT), (rows, narrow)) for bound in bounds]
    kept.wait()
    for copy in copies:
        copy.wait()

    image = [jnp.zeros((rows, narrow), jnp.float32) for _ in range(4)]
    remain = jnp.ones((rows, narrow), jnp.float32)
    for position in range(bricks):
        chosen = order[position]
        value = [
            (held[chosen, c].astype(jnp.float32) + float(LIMIT)) * units[c] for c in range(4)
        ]
        image = [image[c] + remain * value[c] for c in range(4)]
        remain = remain * (1.0 - value[3])
    for c in range(4):
        out[c] = image[c]


def shards(volume, occupied, sample_counts, depth_order, colors, density):
    slices, rows, columns = volume.shape
    bins = colors.shape[1]
    bricks, groups = lax.axis_size("view"), lax.axis_size("img")
    narrow = columns // bricks
    density = density[None, :]
    vmem = pl.BlockSpec(memory_space=pltpu.VMEM)
    smem = pl.BlockSpec(memory_space=pltpu.SMEM)
    first = volume[:, 0:1, :].astype(jnp.float32)
    last = volume[:, rows - 1 : rows, :].astype(jnp.float32)
    nxt, low, high = pl.pallas_call(
        functools.partial(halo_kernel, bricks, groups),
        out_shape=(
            jax.ShapeDtypeStruct((1, rows, columns), volume.dtype),
            jax.ShapeDtypeStruct((slices + 1, 1, columns), jnp.float32),
            jax.ShapeDtypeStruct((slices + 1, 1, columns), jnp.float32),
        ),
        in_specs=[pl.BlockSpec(memory_space=pl.ANY), vmem, vmem],
        out_specs=(vmem,) * 3,
        scratch_shapes=[pltpu.SemaphoreType.DMA((5,)), pltpu.SemaphoreType.DMA((5,))],
        compiler_params=pltpu.CompilerParams(collective_id=0, has_side_effects=True),
        name="halo",
    )(volume, first, last)
    coded = pl.pallas_call(
        functools.partial(march_kernel, bins),
        out_shape=jax.ShapeDtypeStruct((bricks, 4, rows, narrow), jnp.int16),
        in_specs=[smem, smem] + [vmem] * 6,
        out_specs=vmem,
        scratch_shapes=[
            pltpu.VMEM((slices + 1, rows + 2 * PAD, LANES), jnp.float32),
            pltpu.VMEM((slices + 1, rows, LANES), jnp.float32),
        ],
        name="march",
    )(occupied[0, 0], sample_counts[0, 0], volume, nxt, low, high, colors, density)
    return pl.pallas_call(
        functools.partial(blend_kernel, bricks, slices),
        out_shape=jax.ShapeDtypeStruct((4, rows, narrow), jnp.float32),
        in_specs=[smem, vmem, vmem, vmem],
        out_specs=vmem,
        scratch_shapes=[
            pltpu.VMEM((bricks, 4, rows, narrow), jnp.int16),
            pltpu.SemaphoreType.DMA,
            pltpu.SemaphoreType.DMA((bricks,)),
            pltpu.SemaphoreType.DMA((bricks,)),
        ],
        compiler_params=pltpu.CompilerParams(collective_id=1, has_side_effects=True),
        name="blend",
    )(depth_order, coded, colors, density)


def solution(mesh):
    return jax.shard_map(
        shards,
        mesh=mesh,
        in_specs=(
            P("view", "img", None),
            P("view", "img", None),
            P("view", "img", None),
            P(),
            P(),
            P(),
        ),
        out_specs=P(None, "img", "view"),
        check_vma=False,
    )
```

```python
import functools
import math

import jax
import jax.numpy as jnp
from jax import lax
from jax.experimental import pallas as pl
from jax.experimental.pallas import tpu as pltpu
from jax.sharding import PartitionSpec as P

LANES = 128
GROUP = 8
PAD = 8
STRIP = 8
LIMIT = 32767
LEVELS = (4096.0, 4096.0, 4096.0, 65536.0)
SPAN_BITS = 13
SPAN = 1 << SPAN_BITS
CHUNK = 4


LANE_GATHER = lax.GatherDimensionNumbers(
    offset_dims=(),
    collapsed_slice_dims=(1,),
    start_index_map=(1,),
    operand_batching_dims=(0,),
    start_indices_batching_dims=(0,),
)


def gather_lanes(row, index):
    return lax.gather(
        row, index[..., None], LANE_GATHER, (1, 1), mode=lax.GatherScatterMode.PROMISE_IN_BOUNDS
    )


def rounded(value):
    return value.astype(jnp.bfloat16).astype(jnp.float32)


def prepare_tile(tile, vol, nxt, low, high, vals, grads):
    slices, rows, columns = vol.shape
    last = columns // LANES - 1
    starts = [
        pl.multiple_of(jnp.maximum(tile - 1, 0) * LANES, LANES),
        pl.multiple_of(tile * LANES, LANES),
        pl.multiple_of(jnp.minimum(tile + 1, last) * LANES, LANES),
    ]
    source = lax.broadcasted_iota(jnp.int32, (3 * LANES, LANES), 0) - LANES
    target = lax.broadcasted_iota(jnp.int32, (3 * LANES, LANES), 1)
    inside = jnp.logical_and(
        jnp.logical_or(source >= 0, tile > 0), jnp.logical_or(source < LANES, tile < last)
    )
    sign = jnp.where(source == target + 1, 0.5, jnp.where(source == target - 1, -0.5, 0.0))
    weights = jnp.where(inside, sign, 0.0).astype(jnp.bfloat16)
    here = pl.ds(starts[1], LANES)

    def fill(first, count, ref, at):
        blocks = [
            ref[at : at + count, :, pl.ds(start, LANES)].reshape(count * rows, LANES)
            for start in starts
        ]
        along = jnp.dot(
            jnp.concatenate(blocks, axis=1), weights, preferred_element_type=jnp.float32
        ).reshape(count, rows, LANES)
        mid = blocks[1].astype(jnp.float32).reshape(count, rows, LANES)
        for j in range(count):
            z = first + j
            vals[z, PAD : PAD + rows, :] = mid[j] * 0.5
            vals[z, PAD - 1 : PAD, :] = low[z, :, here] * 0.5
            vals[z, PAD + rows : PAD + rows + 1, :] = high[z, :, here] * 0.5
        for j in range(count):
            z = first + j
            across = vals[z, PAD + 1 : PAD + 1 + rows, :] - vals[z, PAD - 1 : PAD - 1 + rows, :]
            grads[z] = (across * across + along[j] * along[j]) * (1.0 / 0.6) + (1.0 / 0.6)

    for first in range(0, slices, CHUNK):
        fill(first, CHUNK, vol, first)
    fill(slices, 1, nxt, 0)


def packed_table(colors, density):
    entries = [colors[c : c + 1, :] for c in range(3)] + [density]
    lane = lax.broadcasted_iota(jnp.int32, (STRIP, LANES), 1)
    pairs = []
    for entry, level in zip(entries, LEVELS):
        whole = (jnp.broadcast_to(entry, (STRIP, LANES)) * level).astype(jnp.int32)
        after = jnp.where(lane == LANES - 1, 0, pltpu.roll(whole, LANES - 1, 1))
        pairs.append(whole * SPAN + after)
    return pairs


def march_tile(samples, pairs, vals, grads, slices, rows, bins):
    inverse = 1.0 / jnp.full((STRIP, LANES), samples.astype(jnp.float32))
    extinct = (-slices * math.log2(math.e) / LEVELS[3]) * inverse
    half = 0.5 * (bins - 1)
    strips = rows // STRIP

    def group(begin, size, carry):
        carry = list(carry)
        for inner in range(size):
            k = begin + inner
            valid = k < samples
            travel = jnp.minimum(k + 1, samples) * slices
            base = jnp.minimum(lax.div(travel, samples), slices - 1)
            part = (travel - base * samples).astype(jnp.float32) * inverse
            rate = jnp.where(valid, 1.0, 0.0) * extinct
            for strip in range(strips):
                red, green, blue, remain = carry[4 * strip : 4 * strip + 4]
                v0 = vals[base, pl.ds(PAD + strip * STRIP, STRIP), :]
                v1 = vals[base + 1, pl.ds(PAD + strip * STRIP, STRIP), :]
                q0 = grads[base, pl.ds(strip * STRIP, STRIP), :]
                q1 = grads[base + 1, pl.ds(strip * STRIP, STRIP), :]
                level = half * jnp.tanh(v0 + part * (v1 - v0)) + half
                shift = q0 + part * (q1 - q0)
                index = level.astype(jnp.int32)
                frac = level - index.astype(jnp.float32)
                upper = rounded(frac)
                lower = rounded(1.0 - frac)
                both = [gather_lanes(pair, index) for pair in pairs]
                found = [lax.shift_right_logical(p, SPAN_BITS).astype(jnp.float32) for p in both]
                found += [lax.bitwise_and(p, SPAN - 1).astype(jnp.float32) for p in both]
                sigma = lower * found[3] + upper * found[7]
                left = remain * jnp.exp2(sigma * rate)
                weight = (remain - left) * (1.0 - 1.0 / shift)
                near = weight * lower
                far = weight * upper
                carry[4 * strip : 4 * strip + 4] = [
                    red + near * found[0] + far * found[4],
                    green + near * found[1] + far * found[5],
                    blue + near * found[2] + far * found[6],
                    left,
                ]
        return tuple(carry)

    zero = jnp.zeros((STRIP, LANES), jnp.float32)
    half_group = GROUP // 2
    wholes = lax.div(samples + (half_group - 1), GROUP)
    begin = wholes * GROUP
    done = lax.fori_loop(
        0,
        wholes,
        lambda number, carry: group(number * GROUP, GROUP, carry),
        (zero, zero, zero, zero + 1.0) * strips,
    )
    rest = (begin < samples).astype(jnp.int32)
    done = lax.fori_loop(0, rest, lambda number, carry: group(begin, half_group, carry), done)
    units = [1.0 / level for level in LEVELS[:3]] + [1.0]
    return [jnp.concatenate(done[c::4], axis=0) * units[c] for c in range(4)]


def channel_bounds(colors, density, slices):
    cover = 1.0 - jnp.exp2(
        (-1.01 * math.log2(math.e) * slices) * jnp.max(density, axis=1, keepdims=True)
    )
    most = jnp.max(colors, axis=1, keepdims=True)
    return [1.01 * cover * (most[c : c + 1] if c < 3 else 1.0) for c in range(4)]


def march_kernel(
    bins, listed, counts, vol, nxt, low, high, colors_ref, density_ref, out, vals, grads
):
    slices, rows, columns = vol.shape
    per = out.shape[3] // LANES
    colors = colors_ref[...].astype(jnp.float32)
    density = density_ref[...].astype(jnp.float32)
    pairs = packed_table(colors, density)
    out[...] = jnp.full(out.shape, -LIMIT, jnp.int16)
    scales = [2.0 * LIMIT / bound for bound in channel_bounds(colors, density, slices)]

    def per_slot(slot, carry):
        tile = listed[slot]

        @pl.when(tile >= 0)
        def _():
            prepare_tile(tile, vol, nxt, low, high, vals, grads)
            red, green, blue, remain = march_tile(
                counts[tile], pairs, vals, grads, slices, rows, bins
            )
            owner = lax.div(tile, per)
            where = pl.ds(pl.multiple_of((tile - owner * per) * LANES, LANES), LANES)
            for c, value in enumerate((red, green, blue, 1.0 - remain)):
                code = (value * scales[c] + 0.5).astype(jnp.int32) - LIMIT
                out[owner, c, :, where] = code.astype(jnp.int16)

        return carry

    lax.fori_loop(0, columns // LANES, per_slot, 0)


def halo_kernel(
    bricks, groups, vol, nxt, low, high, edges, first, last, local, send, recv
):
    b, g = lax.axis_index("view"), lax.axis_index("img")
    slices, rows, columns = vol.shape
    barrier = pltpu.get_barrier_semaphore()
    steps = [(0, 1), (0, -1), (-1, 0), (-1, 1), (-1, -1)]

    def exists(vb, vg):
        return jnp.logical_and(
            jnp.logical_and(b + vb >= 0, b + vb < bricks),
            jnp.logical_and(g + vg >= 0, g + vg < groups),
        )

    met = jnp.int32(0)
    for vb, vg in steps + [(1, 0), (1, 1), (1, -1)]:
        here = exists(vb, vg)

        @pl.when(here)
        def _(vb=vb, vg=vg):
            pl.semaphore_signal(
                barrier, inc=1, device_id=(b + vb, g + vg), device_id_type=pl.DeviceIdType.MESH
            )

        met = met + here.astype(jnp.int32)
    ends = [0, rows - PAD]
    loads = [
        pltpu.make_async_copy(vol.at[:, pl.ds(end, PAD), :], edges.at[i], local.at[i])
        for i, end in enumerate(ends)
    ]
    for load in loads:
        load.start()
    for load in loads:
        load.wait()
    for j in range(slices):
        first[j] = edges[0, j].astype(jnp.float32)[0:1]
        last[j] = edges[1, j].astype(jnp.float32)[PAD - 1 : PAD]
    pl.semaphore_wait(barrier, met)
    main, extra = pl.ds(0, slices), pl.ds(slices, 1)
    plan = [
        (last, low.at[main]),
        (first, high.at[main]),
        (vol.at[pl.ds(0, 1)], nxt),
        (last.at[pl.ds(0, 1)], low.at[extra]),
        (first.at[pl.ds(0, 1)], high.at[extra]),
    ]

    def copy(i):
        (vb, vg), (source, target) = steps[i], plan[i]
        return pltpu.make_async_remote_copy(
            src_ref=source,
            dst_ref=target,
            send_sem=send.at[i],
            recv_sem=recv.at[i],
            device_id=(b + vb, g + vg),
            device_id_type=pl.DeviceIdType.MESH,
        )

    for i, (vb, vg) in enumerate(steps):

        @pl.when(exists(vb, vg))
        def _(i=i):
            copy(i).start()

        @pl.when(jnp.logical_not(exists(-vb, -vg)))
        def _(i=i):
            plan[i][1][...] = jnp.zeros(plan[i][1].shape, plan[i][1].dtype)

    for i, (vb, vg) in enumerate(steps):

        @pl.when(exists(vb, vg))
        def _(i=i):
            copy(i).wait_send()

        @pl.when(exists(-vb, -vg))
        def _(i=i):
            copy(i).wait_recv()


def blend_kernel(bricks, slices, order, mine, colors, density, out, held, local, send, recv):
    b, g = lax.axis_index("view"), lax.axis_index("img")
    barrier = pltpu.get_barrier_semaphore()
    for step in range(1, bricks):
        pl.semaphore_signal(
            barrier,
            inc=1,
            device_id=(lax.rem(b + step, bricks), g),
            device_id_type=pl.DeviceIdType.MESH,
        )
    kept = pltpu.make_async_copy(mine.at[b], held.at[b], local)
    kept.start()
    pl.semaphore_wait(barrier, bricks - 1)
    copies = []
    for step in sorted(range(1, bricks), key=lambda r: (abs(r - bricks // 2), r)):
        peer = lax.rem(b + step, bricks)
        copies.append(
            pltpu.make_async_remote_copy(
                src_ref=mine.at[peer],
                dst_ref=held.at[b],
                send_sem=send.at[step],
                recv_sem=recv.at[step],
                device_id=(peer, g),
                device_id_type=pl.DeviceIdType.MESH,
            )
        )
        copies[-1].start()
    bounds = channel_bounds(
        colors[...].astype(jnp.float32), density[...].astype(jnp.float32), slices
    )
    rows, narrow = out.shape[1:]
    units = [jnp.broadcast_to(bound / (2.0 * LIMIT), (rows, narrow)) for bound in bounds]
    kept.wait()
    for copy in copies:
        copy.wait()

    image = [jnp.zeros((rows, narrow), jnp.float32) for _ in range(4)]
    remain = jnp.ones((rows, narrow), jnp.float32)
    for position in range(bricks):
        chosen = order[position]
        value = [
            (held[chosen, c].astype(jnp.float32) + float(LIMIT)) * units[c] for c in range(4)
        ]
        image = [image[c] + remain * value[c] for c in range(4)]
        remain = remain * (1.0 - value[3])
    for c in range(4):
        out[c] = image[c]


def shards(volume, occupied, sample_counts, depth_order, colors, density):
    slices, rows, columns = volume.shape
    bins = colors.shape[1]
    bricks, groups = lax.axis_size("view"), lax.axis_size("img")
    narrow = columns // bricks
    density = density[None, :]
    vmem = pl.BlockSpec(memory_space=pltpu.VMEM)
    smem = pl.BlockSpec(memory_space=pltpu.SMEM)
    nxt, low, high = pl.pallas_call(
        functools.partial(halo_kernel, bricks, groups),
        out_shape=(
            jax.ShapeDtypeStruct((1, rows, columns), volume.dtype),
            jax.ShapeDtypeStruct((slices + 1, 1, columns), jnp.float32),
            jax.ShapeDtypeStruct((slices + 1, 1, columns), jnp.float32),
        ),
        in_specs=[pl.BlockSpec(memory_space=pl.ANY)],
        out_specs=(vmem,) * 3,
        scratch_shapes=[
            pltpu.VMEM((2, slices, PAD, columns), volume.dtype),
            pltpu.VMEM((slices, 1, columns), jnp.float32),
            pltpu.VMEM((slices, 1, columns), jnp.float32),
            pltpu.SemaphoreType.DMA((2,)),
            pltpu.SemaphoreType.DMA((5,)),
            pltpu.SemaphoreType.DMA((5,)),
        ],
        compiler_params=pltpu.CompilerParams(collective_id=0, has_side_effects=True),
        name="halo",
    )(volume)
    coded = pl.pallas_call(
        functools.partial(march_kernel, bins),
        out_shape=jax.ShapeDtypeStruct((bricks, 4, rows, narrow), jnp.int16),
        in_specs=[smem, smem] + [vmem] * 6,
        out_specs=vmem,
        scratch_shapes=[
            pltpu.VMEM((slices + 1, rows + 2 * PAD, LANES), jnp.float32),
            pltpu.VMEM((slices + 1, rows, LANES), jnp.float32),
        ],
        name="march",
    )(occupied[0, 0], sample_counts[0, 0], volume, nxt, low, high, colors, density)
    return pl.pallas_call(
        functools.partial(blend_kernel, bricks, slices),
        out_shape=jax.ShapeDtypeStruct((4, rows, narrow), jnp.float32),
        in_specs=[smem, vmem, vmem, vmem],
        out_specs=vmem,
        scratch_shapes=[
            pltpu.VMEM((bricks, 4, rows, narrow), jnp.int16),
            pltpu.SemaphoreType.DMA,
            pltpu.SemaphoreType.DMA((bricks,)),
            pltpu.SemaphoreType.DMA((bricks,)),
        ],
        compiler_params=pltpu.CompilerParams(collective_id=1, has_side_effects=True),
        name="blend",
    )(depth_order, coded, colors, density)


def solution(mesh):
    return jax.shard_map(
        shards,
        mesh=mesh,
        in_specs=(
            P("view", "img", None),
            P("view", "img", None),
            P("view", "img", None),
            P(),
            P(),
            P(),
        ),
        out_specs=P(None, "img", "view"),
        check_vma=False,
    )
```
